32 devices in a mesh: groups: 2 (over y), track: 4 (over z), expert: 4 (over x, core).
Axes of the slice: x: 2, y: 2, z: 4, core: 2. Of those that a mesh axis runs over, the one named last changes fastest.
Arguments:
- states: bfloat16 [4, 2048, 2048], P('track', ('groups', 'expert')), parts along dimension 1, may hold values from -3 to 3
- routes: int32 [4, 2048, 2], P('track', ('groups', 'expert')), parts along dimension 1, may hold values from 0 to 3, all different within a row; in each aligned block of 256 rows (0 to 255, 256 to 511, ..., all dimensions but the last counted through in order) at most 256 rows name the same one
- route_gates: float32 [4, 2048, 2], P('track', ('groups', 'expert')), parts along dimension 1, may hold values from 0.2 to 1
- norm_gain: float32 [4, 2048], P('track'), may hold values from 0.1 to 1.9
- w_gate: bfloat16 [4, 4, 2048, 768], P('track', 'expert'), may hold values from -0.125 to 0.125
- w_up: bfloat16 [4, 4, 2048, 768], P('track', 'expert'), may hold values from -0.125 to 0.125
- w_down: bfloat16 [4, 4, 768, 2048], P('track', 'expert'), may hold values from -0.21875 to 0.21875
Outputs:
- mixed: bfloat16 [2048, 2048], P(('groups', 'expert'), 'track'), parts along dimension 0
The draws below stay inside these ranges and needn't reach their ends.
There are 2 independent parts, one for each index of `groups`. The reference program is written for one: setup_inputs(seed, part) draws one part's arguments, and reference() takes and returns one part's arrays. A program takes and returns all parts, laid end to end along the dimension named above; an argument that names none is the same for every part. Nothing has to cross between parts.
Inputs may be any that keep to these rules, and one draw needn't show every extreme that they name: `routes`: each token names 2 different experts of its track. Within each track, among the 256 tokens of one index of expert (aligned blocks of the token dimension), no expert is named by more than 256 tokens, and in every draw some expert is named by exactly 256 tokens of some block.
All inputs are finite; a program needn't handle non-finite values.
Results may differ from the reference program's by a relative error of at most 0.023.
Values may be sent and summed in bfloat16 or wider, within the bound.
No kernel may reach another device: no remote copies, remote signals or barrier semaphores. Data moves between devices by JAX's collectives and lax.ppermute only.
A program may use at most 64 MiB of HBM per device.

```python
import math
import jax
import jax.numpy as jnp
import numpy as np
from jax import lax

D = 2048
FF = 768
TOP = 2
TOK_DEV = 256
TRACKS = 4
EXPERTS = 4
TOKENS = 1024
CAP = 256
N_EXPERT = 4


def block_levels(rng, shape, cuts, smallest, largest):
    factor_of = 1.0
    for axis_at, shards_of in cuts:
        draws = jax.random.uniform(jax.random.fold_in(jax.random.fold_in(rng, 6), axis_at), (shards_of,), jnp.float32, smallest / len(cuts), largest / len(cuts))
        factor_of = factor_of * jnp.repeat(jnp.exp(draws), shape[axis_at] // shards_of).reshape((-1,) + (1,) * (len(shape) - 1 - axis_at))
    return factor_of


def assign_block(stream_key, own, number, rows, number_of, top, most, skew):
    sequence = jax.random.permutation(stream_key, number_of)
    packed, ordinary = load_shares(number_of, rows * top, most, skew, True), load_shares(number_of, rows * top, most, skew, False)
    places = jnp.arange(number_of)

    def named(tallies, turn):
        used = int((tallies > 0).sum())
        fixed = max(1, used // 4)
        moved = fixed + (places - fixed + turn * (used - fixed)) % max(1, number_of - fixed)
        return jnp.zeros((number_of,), jnp.int32).at[sequence[jnp.where(places < fixed, places, moved)]].set(jnp.asarray(tallies, jnp.int32))

    tallies = jnp.where(number % 4 == 0, named(packed, number // 4), named(ordinary, number - number // 4 - 1))
    mixed = jax.random.permutation(jax.random.fold_in(own, 3), number_of)
    donor, sink = mixed[0:number_of // 2 * 2:2], mixed[1:number_of // 2 * 2:2]
    margin = jnp.minimum(tallies[donor] - 1, most - tallies[sink]) // 2
    margin = jnp.where((donor == sequence[0]) | (sink == sequence[0]) | (tallies[sink] == 0), 0, jnp.maximum(margin, 0))
    moved = jax.random.randint(jax.random.fold_in(own, 4), (number_of // 2,), 0, 1 << 20) % (margin + 1)
    tallies = tallies.at[donor].add(-moved).at[sink].add(moved)
    items = jnp.searchsorted(jnp.cumsum(tallies), jnp.arange(rows * top), side="right").astype(jnp.int32)
    grid = items.reshape(top, rows).T
    grid = grid[jax.random.permutation(jax.random.fold_in(own, 1), rows)]
    turn = jax.random.randint(jax.random.fold_in(own, 2), (rows, 1), 0, top)
    return jnp.take_along_axis(grid, (jnp.arange(top)[None, :] + turn) % top, axis=1)


def load_shares(number_of, total, reach, slope, full):
    weights = [(1 << 20) // math.isqrt(grade ** slope) + 1 for grade in range(1, number_of + 1)]
    largest = reach if full else min(reach, max(-(-total // number_of), total * weights[0] // sum(weights)))
    least = 1 if total - largest >= number_of - 1 else 0
    given, spare = [largest] + [least] * (number_of - 1), total - largest - least * (number_of - 1)
    while spare > 0:
        movable = [i for i in range(1, number_of) if given[i] < largest] or [i for i in range(1, number_of) if given[i] < reach]
        mass, left = sum([weights[i] for i in movable]), spare
        for i in movable:
            more = min(reach - given[i], max(1, left * weights[i] // mass), spare)
            given[i] = given[i] + more
            spare = spare - more
    return np.array(given)


def centred(own_key, dims, scale, limit, cuts=(), kind=jnp.bfloat16):
    result = jax.random.normal(own_key, dims, jnp.float32) * scale
    if len(cuts) > 0:
        result = block_levels(own_key, dims, cuts, -0.22, 0.18) * result
    return jnp.clip(result, min=-limit, max=limit).astype(kind)


def setup_inputs(seed: int = 0, part: int = 0) -> dict:
    arg_keys = jax.random.split(jax.random.key(seed), 8)
    own_keys = jax.random.split(jax.random.fold_in(arg_keys[7], part), 8)
    states = centred(own_keys[0], (TRACKS, TOKENS, D), 0.5, 3.0, ((0, 4), (1, 4)))
    routes_keys = jax.random.split(jax.random.fold_in(own_keys[1], 1), TRACKS * TOKENS // TOK_DEV)
    routes_turns = jax.random.permutation(jax.random.fold_in(own_keys[1], 3), TRACKS * TOKENS // TOK_DEV)
    routes = jax.vmap(lambda own, number: assign_block(jax.random.fold_in(own_keys[1], 2), own, number, TOK_DEV, EXPERTS, TOP, CAP, 2))(routes_keys, routes_turns).reshape((TRACKS, TOKENS, TOP))
    route_gates = jnp.clip(0.2 + 0.8 * jax.random.uniform(own_keys[2], (TRACKS, TOKENS, TOP), jnp.float32) ** block_levels(own_keys[2], (TRACKS, TOKENS, TOP), ((0, 4), (1, 4)), -0.2, 0.2), 0.2, 1.0)
    norm_gain = jnp.clip(1.0 + 0.18 * jax.random.normal(arg_keys[3], (TRACKS, D), jnp.float32), 0.1, 1.9)
    w_gate = centred(arg_keys[4], (TRACKS, EXPERTS, D, FF), D ** -0.5, 0.125, ((0, 4), (1, 4)))
    w_up = centred(arg_keys[5], (TRACKS, EXPERTS, D, FF), D ** -0.5, 0.125, ((0, 4), (1, 4)))
    w_down = centred(arg_keys[6], (TRACKS, EXPERTS, FF, D), FF ** -0.5, 0.21875, ((0, 4), (1, 4)))
    return dict(states=states, routes=routes, route_gates=route_gates, norm_gain=norm_gain, w_gate=w_gate, w_up=w_up, w_down=w_down)


def slot_places(chosen, experts, capacity):
    flat_ids = chosen.reshape(-1)
    labels = jnp.arange(experts, dtype=jnp.int32)
    matches = (flat_ids[:, None] == labels[None, :]).astype(jnp.int32)
    earlier = jnp.cumsum(matches, axis=0) - matches
    slot_index = lax.optimization_barrier(jnp.sum(earlier * matches, axis=1))
    return flat_ids * capacity + slot_index

def block_places(chosen):
    return slot_places(chosen, EXPERTS, CAP)

def reference(states, routes, route_gates, norm_gain, w_gate, w_up, w_down):
    summed_entry = lax.optimization_barrier(jnp.sum(states.astype(jnp.float32), axis=0))
    inverse_rms = lax.rsqrt(lax.optimization_barrier(jnp.mean(summed_entry * summed_entry, axis=1, keepdims=True)) + 1e-06)
    unit_rows = summed_entry * inverse_rms
    blocks = jnp.arange(N_EXPERT, dtype=jnp.int32)

    def one_track(carry, pieces):
        gain, chosen, gates, gate_w, up_w, down_w = pieces
        normed = (unit_rows * gain[None, :]).astype(jnp.bfloat16)
        grouped = chosen.reshape(N_EXPERT, TOK_DEV, TOP)
        local_places = jax.vmap(block_places)(grouped)
        expert_ids = grouped.reshape(N_EXPERT, TOP * TOK_DEV)
        slot_index = local_places - expert_ids * CAP
        positions = (expert_ids * N_EXPERT + blocks[:, None]) * CAP + slot_index
        source_rows = blocks[:, None] * TOK_DEV + jnp.arange(TOP * TOK_DEV, dtype=jnp.int32)[None, :] // TOP
        row_owner = jnp.full((EXPERTS * N_EXPERT * CAP,), TOKENS, jnp.int32)
        row_owner = row_owner.at[positions.reshape(-1)].set(source_rows.reshape(-1))
        buffer = jnp.take(normed, row_owner, axis=0, mode='fill', fill_value=0).reshape(EXPERTS, N_EXPERT * CAP, D)
        buffer_wide = buffer.astype(jnp.float32)
        gate_part = jnp.einsum('end,edf->enf', buffer_wide, gate_w.astype(jnp.float32))
        up_part = jnp.einsum('end,edf->enf', buffer_wide, up_w.astype(jnp.float32))
        hidden = (jax.nn.silu(gate_part) * up_part).astype(jnp.bfloat16)
        expert_out = jnp.einsum('enf,efd->end', hidden.astype(jnp.float32), down_w.astype(jnp.float32)).astype(jnp.bfloat16)
        picked = jnp.take(expert_out.reshape(-1, D), positions.reshape(-1), axis=0).astype(jnp.float32)
        branch = lax.optimization_barrier(jnp.sum(picked.reshape(TOKENS, TOP, D) * gates[:, :, None], axis=1))
        return (carry + branch, None)
    start = jnp.zeros((TOKENS, D), jnp.float32)
    summed, unused = lax.scan(one_track, start, (norm_gain, routes, route_gates, w_gate, w_up, w_down))
    return (summed_entry + summed).astype(jnp.bfloat16)
```

```python
import functools

import jax
import jax.numpy as jnp
from jax import lax
from jax.experimental import pallas as pl
from jax.experimental.pallas import tpu as pltpu
from jax.sharding import PartitionSpec as P

CHUNKS = (1, 1, 1, 1)
HOP, WIRE, EXPERT = 2.2, 22.5, 20.0


def slot_places(chosen, experts, capacity):
    flat_ids = chosen.reshape(-1)
    labels = jnp.arange(experts, dtype=jnp.int32)
    matches = (flat_ids[:, None] == labels[None, :]).astype(jnp.int32)
    earlier = jnp.cumsum(matches, axis=0) - matches
    slot_index = jnp.sum(earlier * matches, axis=1)
    return flat_ids * capacity + slot_index


def expert_hidden(arrived, gate_w, up_w, exp_dev):
    sources = arrived.shape[0] // exp_dev
    grouped = arrived.reshape(sources, exp_dev, arrived.shape[1], arrived.shape[2])
    gate_part = jnp.einsum("secd,edf->secf", grouped, gate_w, preferred_element_type=jnp.float32)
    up_part = jnp.einsum("secd,edf->secf", grouped, up_w, preferred_element_type=jnp.float32)
    return (jax.nn.silu(gate_part) * up_part).astype(jnp.bfloat16)


def dispatched(states, routes, route_gates, norm_gain, w_gate, w_up, w_down):
    summed_entry = lax.psum(states[0], "track").astype(jnp.float32)
    tok_rows, model_width = summed_entry.shape
    top_count = routes.shape[2]
    exp_dev = w_gate.shape[1]
    experts = exp_dev * lax.axis_size("expert")
    tracks = lax.axis_size("track")
    capacity = 4 * tok_rows // experts
    slice_width = model_width // tracks
    inverse_rms = lax.rsqrt(jnp.mean(summed_entry * summed_entry, axis=1, keepdims=True) + 1e-06)
    normed = (summed_entry * inverse_rms * norm_gain[0][None, :]).astype(jnp.bfloat16)
    places = slot_places(routes[0], experts, capacity)
    row_owner = jnp.full((experts * capacity,), tok_rows, jnp.int32)
    row_owner = row_owner.at[places].set(
        jnp.arange(top_count * tok_rows, dtype=jnp.int32) // top_count
    )
    outbound = jnp.take(normed, row_owner, axis=0, mode="fill", fill_value=0).reshape(
        experts, capacity, model_width
    )
    own_slice = lax.dynamic_slice_in_dim(
        summed_entry, lax.axis_index("track") * slice_width, slice_width, 1
    )
    arrived = lax.all_to_all(outbound, "expert", split_axis=0, concat_axis=0, tiled=True)
    count_items = arrived.shape[1]
    hidden = expert_hidden(arrived, w_gate[0], w_up[0], exp_dev)
    result = jnp.einsum(
        "secf,efd->secd", hidden, w_down[0], preferred_element_type=jnp.float32
    ).astype(jnp.bfloat16)
    returned = lax.all_to_all(
        result.reshape(experts, count_items, model_width),
        "expert",
        split_axis=0,
        concat_axis=0,
        tiled=True,
    )
    picked = jnp.take(returned.reshape(-1, model_width), places, axis=0)
    branch = jnp.sum(
        picked.reshape(tok_rows, top_count, model_width) * route_gates[0][:, :, None], axis=1
    )
    summed = lax.psum_scatter(
        branch.astype(jnp.bfloat16), "track", scatter_dimension=1, tiled=True
    ).astype(jnp.float32)
    return (own_slice + summed).astype(jnp.bfloat16)


def swap(value, axis, bit):
    size = lax.axis_size(axis)
    return lax.ppermute(value, axis, [(i, i ^ bit) for i in range(size)])


def bits_of(size):
    out, bit = [], 1
    while bit < size:
        out.append(bit)
        bit *= 2
    return out


VMEM = pl.BlockSpec(memory_space=pltpu.VMEM)
SMEM = pl.BlockSpec(memory_space=pltpu.SMEM)
ANY = pl.BlockSpec(memory_space=pl.ANY)


def call(body, outs, ins, scalars, extra, scratch=(), limit=4):
    count = 1 + len(ins)

    def kernel(*refs):
        body(*refs[:count], *refs[count + len(extra) :])

    return pl.pallas_call(
        kernel,
        out_shape=outs,
        in_specs=[SMEM] + [VMEM] * len(ins) + [ANY] * len(extra),
        out_specs=[VMEM] * len(outs),
        scratch_shapes=scratch,
        compiler_params=pltpu.CompilerParams(vmem_limit_bytes=limit * 1024 * 1024),
    )(scalars, *ins, *extra)


def half_of(*shape):
    return jax.ShapeDtypeStruct(shape, jnp.bfloat16)


def full_of(*shape):
    return jax.ShapeDtypeStruct(shape, jnp.float32)


def add_body(where, *refs):
    total = refs[0][...].astype(jnp.float32)
    for ref in refs[1:-1]:
        total = total + ref[...].astype(jnp.float32)
    refs[-1][...] = total.astype(jnp.bfloat16)


def pick_body(step, where, mine, came, out):
    takes = where[1] == step
    out[...] = jnp.where(takes, came[...], mine[...])


def tile_of(size, want):
    while size % want:
        want //= 2
    return want


def split_body(where, whole, *parts):
    start = 0
    for part in parts:
        part[...] = whole[start : start + part.shape[0]]
        start += part.shape[0]


def expert_body(piece, first, where, sources, gain, weight, gates, ups, downs, keep, send, normed, hidden):
    rows = sources[0].shape[0]
    ff = gates[0].shape[1]
    for place, ref in enumerate(sources):
        wide = ref[...].astype(jnp.float32)
        inverse = lax.rsqrt(jnp.mean(wide * wide, axis=1, keepdims=True) + 1e-06)
        normed[place * rows : (place + 1) * rows] = (wide * inverse * gain[...]).astype(jnp.bfloat16)
    block = tile_of(ff, 256)
    chosen = jnp.concatenate([part[first : first + rows] for part in weight], axis=0)
    for expert, (gate, up) in enumerate(zip(gates, ups)):

        def hide(step, carry, expert=expert, gate=gate, up=up):
            at = pl.ds(pl.multiple_of(step * block, block), block)
            gate_part = jnp.dot(normed[...], gate[:, at], preferred_element_type=jnp.float32)
            up_part = jnp.dot(normed[...], up[:, at], preferred_element_type=jnp.float32)
            value = jax.nn.silu(gate_part) * up_part * chosen[:, expert : expert + 1]
            to = pl.ds(pl.multiple_of(expert * ff + step * block, block), block)
            hidden[:, to] = value.astype(jnp.bfloat16)
            return carry

        lax.fori_loop(0, ff // block, hide, 0)
    parity = where[0] % 2
    for side, out in ((1 - parity, send), (parity, keep)):

        def lower(step, carry, side=side, out=out):
            at = pl.ds(pl.multiple_of((2 * step + side) * piece, piece), piece)
            value = jnp.dot(hidden[:, :ff], downs[0][:, at], preferred_element_type=jnp.float32)
            for expert in range(1, len(downs)):
                value += jnp.dot(
                    hidden[:, expert * ff : (expert + 1) * ff],
                    downs[expert][:, at],
                    preferred_element_type=jnp.float32,
                )
            to = pl.ds(pl.multiple_of(step * piece, piece), piece)
            out[:, to] = value.astype(out.dtype)
            return carry

        lax.fori_loop(0, out.shape[1] // piece, lower, 0)


def split_columns_body(bit, piece, where, kept, came, keep, send):
    parity = (where[0] // bit) % 2
    for step in range(keep.shape[1] // piece):
        to = slice(step * piece, (step + 1) * piece)
        for side, out in ((1 - parity, send), (parity, keep)):
            at = pl.ds(pl.multiple_of((2 * step + side) * piece, piece), piece)
            out[:, to] = (kept[:, at] + came[:, at].astype(jnp.float32)).astype(out.dtype)


def split_rows_body(where, kept, came, keep, send):
    rows = keep.shape[0]
    keep[...] = kept[:rows] + came[:rows].astype(jnp.float32)
    send[...] = (kept[rows:] + came[rows:].astype(jnp.float32)).astype(jnp.bfloat16)


def final_body(piece, starts, mine, where, kept, came, base, *refs):
    out = refs[-1]
    rows = kept.shape[0]
    at = pl.ds(pl.multiple_of(where[0] * piece, piece), piece)
    total = kept[...] + came[...].astype(jnp.float32) + base[:, at].astype(jnp.float32)
    out[starts[mine] : starts[mine] + rows] = total.astype(out.dtype)
    for place, ref in zip((c for c in range(len(starts)) if c != mine), refs[:-1]):
        out[starts[place] : starts[place] + ref.shape[0]] = ref[...]


def dense(states, routes, route_gates, norm_gain, w_gate, w_up, w_down):
    tok_rows, width = states.shape[1:]
    ff = w_gate.shape[3]
    experts, tracks = lax.axis_size("expert"), lax.axis_size("track")
    me_e, me_t = lax.axis_index("expert"), lax.axis_index("track")
    middle = tracks // 2
    ring = jnp.where(me_t < middle, middle - 1 - me_t, me_t - middle)
    where = jnp.stack([me_t, ring]).astype(jnp.int32)
    piece = width // tracks
    far_bits = list(reversed(bits_of(experts)))[:-1]
    near = bits_of(experts)[0]
    groups = 2 ** len(far_bits)

    sizes = [tok_rows * part // sum(CHUNKS) for part in CHUNKS]
    starts = [sum(sizes[:c]) for c in range(len(sizes))]
    to_vmem = lambda value: pltpu.with_memory_space_constraint(value, pltpu.VMEM)

    weights = [
        (to_vmem(value[0, 0]), to_vmem(swap(value[0, 0], "expert", near)))
        for value in (w_gate, w_up, w_down)
    ]

    labels = jnp.arange(experts, dtype=jnp.int32)
    table = jnp.sum(
        jnp.where(routes[0][None] == labels[:, None, None], route_gates[0][None], 0.0), axis=2
    )[:, None]
    for bit in far_bits:
        table = jnp.concatenate([table, swap(table, "expert", bit)], axis=1)
    chosen = jnp.stack(
        [lax.dynamic_index_in_dim(table, me, 0, keepdims=False) for me in (me_e, me_e ^ near)],
        axis=2,
    )

    chosen = [chosen[group] for group in range(groups)]
    last = [chosen[0]]

    def run(body, outs, ins, **options):
        got = call(body, outs, ins, where, last[:1], **options)
        last[0] = got[-1]
        return got

    pieces = call(split_body, [half_of(size, width) for size in sizes], [states[0]], where, [])

    inward = lambda s: [(s, s + 1), (tracks - 1 - s, tracks - 2 - s)]
    outward = lambda s: [(s, s - 1), (tracks - 1 - s, tracks - s)]
    across = [(middle - 1, middle), (middle, middle - 1)]

    stages = []
    state = [dict() for _ in sizes]
    result = [None]

    def begin(c):
        own = pieces[c]
        state[c]["sum"] = [own]
        state[c]["came"] = lax.ppermute(own, "track", inward(0) if middle > 1 else across)

    def gather(c, step):
        st = state[c]
        st["sum"].append(st["came"])
        (total,) = run(add_body, [half_of(sizes[c], width)], st["sum"])
        if step < middle - 1:
            link = inward(step + 1) if step + 1 < middle - 1 else across
            st["came"] = lax.ppermute(total, "track", link)
        else:
            st["total"] = total
            spread(c, middle - 1)

    def spread(c, step):
        st = state[c]
        if step > 0:
            st["came"] = lax.ppermute(st["total"], "track", outward(step))
        else:
            rows = st["total"]
            parts = [rows]
            for bit in far_bits:
                parts += [swap(value, "expert", bit) for value in parts]
            st["parts"] = parts

    def picked(c, step):
        st = state[c]
        away = middle - step
        (st["total"],) = run(
            functools.partial(pick_body, away),
            [half_of(sizes[c], width)],
            [st["total"], st["came"]],
        )
        spread(c, step - 1)

    def expert(c):
        st = state[c]
        rows = sizes[c] * groups
        gates, ups, downs = weights

        def body(where, *refs):
            sources, refs = refs[:groups], refs[groups:]
            picks, refs = refs[:groups], refs[groups:]
            expert_body(
                piece, starts[c], where, sources, refs[0], picks, refs[1:3], refs[3:5], refs[5:7], *refs[7:]
            )

        st["keep"], send = run(
            body,
            [full_of(rows, width // 2), half_of(rows, width // 2)],
            [*st["parts"], *chosen, norm_gain, *gates, *ups, *downs],
            scratch=[pltpu.VMEM((rows, width), jnp.bfloat16), pltpu.VMEM((rows, 2 * ff), jnp.bfloat16)],
            limit=26,
        )
        st["came"] = swap(send, "track", 1)

    def columns(c, bit):
        st = state[c]
        rows, count = st["keep"].shape
        st["keep"], send = run(
            functools.partial(split_columns_body, bit, piece),
            [full_of(rows, count // 2), half_of(rows, count // 2)],
            [st["keep"], st["came"]],
        )
        st["came"] = swap(send, "track", bit)

    def rows_of(c, bit):
        st = state[c]
        rows, count = st["keep"].shape
        st["keep"], send = run(
            split_rows_body,
            [full_of(rows // 2, count), half_of(rows // 2, count)],
            [st["keep"], st["came"]],
        )
        st["came"] = swap(send, "expert", bit)

    def final(c):
        st = state[c]
        ins = [st["keep"], st["came"], st["total"]]
        others = [other.get("out") for other in state if other is not st]
        if any(other is None for other in others):
            body = functools.partial(final_body, piece, (0,), 0)
            (st["out"],) = run(body, [half_of(sizes[c], piece)], ins)
        else:
            body = functools.partial(final_body, piece, starts, c)
            (result[0],) = run(body, [half_of(tok_rows, piece)], ins + others)

    events = []
    for c in range(len(sizes)):
        wire = starts[c] / tok_rows * WIRE
        own_wire = sizes[c] / tok_rows * WIRE
        hop = HOP + own_wire
        now = wire
        for step in range(middle):
            now += hop
            events.append((now, functools.partial(gather, c, step)))
        for step in range(middle - 1, 0, -1):
            now += hop
            events.append((now, functools.partial(picked, c, step)))
        now += hop * max(1, len(far_bits))
        events.append((now, functools.partial(expert, c)))
        now += EXPERT * sizes[c] / tok_rows
        for bit in bits_of(tracks)[1:]:
            now += hop
            events.append((now, functools.partial(columns, c, bit)))
        now += hop
        for bit in reversed(far_bits):
            events.append((now, functools.partial(rows_of, c, bit)))
            now += HOP + own_wire / 4
        events.append((now, functools.partial(final, c)))
    for c in range(len(sizes)):
        begin(c)
    for _, event in sorted(events, key=lambda item: item[0]):
        event()
    return result[0]


def local(states, routes, route_gates, norm_gain, w_gate, w_up, w_down):
    tok_rows = states.shape[1]
    experts = w_gate.shape[1] * lax.axis_size("expert")
    if 4 * tok_rows // experts < tok_rows or w_gate.shape[1] != 1:
        return dispatched(states, routes, route_gates, norm_gain, w_gate, w_up, w_down)
    return dense(states, routes, route_gates, norm_gain, w_gate, w_up, w_down)


def solution(mesh):
    return jax.shard_map(
        local,
        mesh=mesh,
        in_specs=(
            P("track", ("groups", "expert"), None),
            P("track", ("groups", "expert"), None),
            P("track", ("groups", "expert"), None),
            P("track", None),
            P("track", "expert", None, None),
            P("track", "expert", None, None),
            P("track", "expert", None, None),
        ),
        out_specs=P(("groups", "expert"), "track"),
        check_vma=False,
    )
```

```python
import functools

import jax
import jax.numpy as jnp
from jax import lax
from jax.experimental import pallas as pl
from jax.experimental.pallas import tpu as pltpu
from jax.sharding import PartitionSpec as P

CHUNKS = (1, 1, 1, 1)
HOP, WIRE, EXPERT = 2.2, 22.5, 20.0


def slot_places(chosen, experts, capacity):
    flat_ids = chosen.reshape(-1)
    labels = jnp.arange(experts, dtype=jnp.int32)
    matches = (flat_ids[:, None] == labels[None, :]).astype(jnp.int32)
    earlier = jnp.cumsum(matches, axis=0) - matches
    slot_index = jnp.sum(earlier * matches, axis=1)
    return flat_ids * capacity + slot_index


def expert_hidden(arrived, gate_w, up_w, exp_dev):
    sources = arrived.shape[0] // exp_dev
    grouped = arrived.reshape(sources, exp_dev, arrived.shape[1], arrived.shape[2])
    gate_part = jnp.einsum("secd,edf->secf", grouped, gate_w, preferred_element_type=jnp.float32)
    up_part = jnp.einsum("secd,edf->secf", grouped, up_w, preferred_element_type=jnp.float32)
    return (jax.nn.silu(gate_part) * up_part).astype(jnp.bfloat16)


def dispatched(states, routes, route_gates, norm_gain, w_gate, w_up, w_down):
    summed_entry = lax.psum(states[0], "track").astype(jnp.float32)
    tok_rows, model_width = summed_entry.shape
    top_count = routes.shape[2]
    exp_dev = w_gate.shape[1]
    experts = exp_dev * lax.axis_size("expert")
    tracks = lax.axis_size("track")
    capacity = 4 * tok_rows // experts
    slice_width = model_width // tracks
    inverse_rms = lax.rsqrt(jnp.mean(summed_entry * summed_entry, axis=1, keepdims=True) + 1e-06)
    normed = (summed_entry * inverse_rms * norm_gain[0][None, :]).astype(jnp.bfloat16)
    places = slot_places(routes[0], experts, capacity)
    row_owner = jnp.full((experts * capacity,), tok_rows, jnp.int32)
    row_owner = row_owner.at[places].set(
        jnp.arange(top_count * tok_rows, dtype=jnp.int32) // top_count
    )
    outbound = jnp.take(normed, row_owner, axis=0, mode="fill", fill_value=0).reshape(
        experts, capacity, model_width
    )
    own_slice = lax.dynamic_slice_in_dim(
        summed_entry, lax.axis_index("track") * slice_width, slice_width, 1
    )
    arrived = lax.all_to_all(outbound, "expert", split_axis=0, concat_axis=0, tiled=True)
    count_items = arrived.shape[1]
    hidden = expert_hidden(arrived, w_gate[0], w_up[0], exp_dev)
    result = jnp.einsum(
        "secf,efd->secd", hidden, w_down[0], preferred_element_type=jnp.float32
    ).astype(jnp.bfloat16)
    returned = lax.all_to_all(
        result.reshape(experts, count_items, model_width),
        "expert",
        split_axis=0,
        concat_axis=0,
        tiled=True,
    )
    picked = jnp.take(returned.reshape(-1, model_width), places, axis=0)
    branch = jnp.sum(
        picked.reshape(tok_rows, top_count, model_width) * route_gates[0][:, :, None], axis=1
    )
    summed = lax.psum_scatter(
        branch.astype(jnp.bfloat16), "track", scatter_dimension=1, tiled=True
    ).astype(jnp.float32)
    return (own_slice + summed).astype(jnp.bfloat16)


def swap(value, axis, bit):
    size = lax.axis_size(axis)
    return lax.ppermute(value, axis, [(i, i ^ bit) for i in range(size)])


def bits_of(size):
    out, bit = [], 1
    while bit < size:
        out.append(bit)
        bit *= 2
    return out


VMEM = pl.BlockSpec(memory_space=pltpu.VMEM)
ANY = pl.BlockSpec(memory_space=pl.ANY)


def call(body, outs, ins, extra=(), scratch=(), limit=4, space=VMEM):
    count = len(ins)

    def kernel(*refs):
        body(*refs[:count], *refs[count + len(extra) :])

    return pl.pallas_call(
        kernel,
        out_shape=outs,
        in_specs=[space] * len(ins) + [ANY] * len(extra),
        out_specs=[VMEM] * len(outs),
        scratch_shapes=scratch,
        compiler_params=pltpu.CompilerParams(vmem_limit_bytes=limit * 1024 * 1024),
    )(*ins, *extra)


def half_of(*shape):
    return jax.ShapeDtypeStruct(shape, jnp.bfloat16)


def full_of(*shape):
    return jax.ShapeDtypeStruct(shape, jnp.float32)


def add_body(*refs):
    total = refs[0][...].astype(jnp.float32)
    for ref in refs[1:-1]:
        total = total + ref[...].astype(jnp.float32)
    refs[-1][...] = total.astype(jnp.bfloat16)


def pick_body(step, mine, came, out):
    tracks, me = lax.axis_size("track"), lax.axis_index("track")
    takes = (me == step) | (me == tracks - 1 - step)
    out[...] = jnp.where(takes, came[...], mine[...])


def tile_of(size, want):
    while size % want:
        want //= 2
    return want


def table_body(routes, gates, out):
    for expert in range(out.shape[0]):
        named = jnp.where(routes[...] == expert, gates[...], 0.0)
        out[expert : expert + 1] = jnp.sum(named, axis=0, keepdims=True)


def turn_body(near, *refs):
    out = refs[-1]
    me = lax.axis_index("expert")
    for place, ref in enumerate(refs[:-1]):
        table = ref[...]
        rows = table.shape[1]
        labels = lax.broadcasted_iota(jnp.int32, table.shape, 0)
        picked = [
            jnp.sum(jnp.where(labels == named, table, 0.0), axis=0, keepdims=True)
            for named in (me, me ^ near)
        ]
        wide = jnp.concatenate(picked + [jnp.zeros((6, rows), jnp.float32)], axis=0)
        out[place] = jnp.transpose(wide)


def split_body(whole, *refs):
    parts, sems = refs[:-1], refs[-1]
    copies, start = [], 0
    for place, part in enumerate(parts):
        copies.append(
            pltpu.make_async_copy(whole.at[start : start + part.shape[0]], part, sems.at[place])
        )
        copies[-1].start()
        start += part.shape[0]
    for copy in copies:
        copy.wait()


def expert_body(piece, first, sources, gain, weight, gates, ups, downs, keep, send, normed, hidden):
    rows = sources[0].shape[0]
    ff = gates[0].shape[1]
    for place, ref in enumerate(sources):
        wide = ref[...].astype(jnp.float32)
        inverse = lax.rsqrt(jnp.mean(wide * wide, axis=1, keepdims=True) + 1e-06)
        normed[place * rows : (place + 1) * rows] = (wide * inverse * gain[...]).astype(jnp.bfloat16)
    block = tile_of(ff, 256)
    chosen = jnp.concatenate(
        [weight[place, first : first + rows] for place in range(len(sources))], axis=0
    )
    for expert, (gate, up) in enumerate(zip(gates, ups)):

        def hide(step, carry, expert=expert, gate=gate, up=up):
            at = pl.ds(pl.multiple_of(step * block, block), block)
            gate_part = jnp.dot(normed[...], gate[:, at], preferred_element_type=jnp.float32)
            up_part = jnp.dot(normed[...], up[:, at], preferred_element_type=jnp.float32)
            value = jax.nn.silu(gate_part) * up_part * chosen[:, expert : expert + 1]
            to = pl.ds(pl.multiple_of(expert * ff + step * block, block), block)
            hidden[:, to] = value.astype(jnp.bfloat16)
            return carry

        lax.fori_loop(0, ff // block, hide, 0, unroll=True)
    parity = lax.axis_index("track") % 2
    for side, out in ((1 - parity, send), (parity, keep)):

        def lower(step, carry, side=side, out=out):
            at = pl.ds(pl.multiple_of((2 * step + side) * piece, piece), piece)
            value = jnp.dot(hidden[:, :ff], downs[0][:, at], preferred_element_type=jnp.float32)
            for expert in range(1, len(downs)):
                value += jnp.dot(
                    hidden[:, expert * ff : (expert + 1) * ff],
                    downs[expert][:, at],
                    preferred_element_type=jnp.float32,
                )
            to = pl.ds(pl.multiple_of(step * piece, piece), piece)
            out[:, to] = value.astype(out.dtype)
            return carry

        lax.fori_loop(0, out.shape[1] // piece, lower, 0, unroll=True)


def split_columns_body(bit, piece, kept, came, keep, send):
    parity = (lax.axis_index("track") // bit) % 2
    for step in range(keep.shape[1] // piece):
        to = slice(step * piece, (step + 1) * piece)
        for side, out in ((1 - parity, send), (parity, keep)):
            at = pl.ds(pl.multiple_of((2 * step + side) * piece, piece), piece)
            out[:, to] = (kept[:, at] + came[:, at].astype(jnp.float32)).astype(out.dtype)


def split_rows_body(kept, came, keep, send):
    rows = keep.shape[0]
    keep[...] = kept[:rows] + came[:rows].astype(jnp.float32)
    send[...] = (kept[rows:] + came[rows:].astype(jnp.float32)).astype(jnp.bfloat16)


def final_body(piece, starts, mine, kept, came, base, *refs):
    out = refs[-1]
    rows = kept.shape[0]
    at = pl.ds(pl.multiple_of(lax.axis_index("track") * piece, piece), piece)
    total = kept[...] + came[...].astype(jnp.float32) + base[:, at].astype(jnp.float32)
    out[starts[mine] : starts[mine] + rows] = total.astype(out.dtype)
    for place, ref in zip((c for c in range(len(starts)) if c != mine), refs[:-1]):
        out[starts[place] : starts[place] + ref.shape[0]] = ref[...]


def dense(states, routes, route_gates, norm_gain, w_gate, w_up, w_down):
    tok_rows, width = states.shape[1:]
    ff = w_gate.shape[3]
    experts, tracks = lax.axis_size("expert"), lax.axis_size("track")
    middle = tracks // 2
    piece = width // tracks
    far_bits = list(reversed(bits_of(experts)))[:-1]
    near = bits_of(experts)[0]
    groups = 2 ** len(far_bits)

    sizes = [tok_rows * part // sum(CHUNKS) for part in CHUNKS]
    starts = [sum(sizes[:c]) for c in range(len(sizes))]
    to_vmem = lambda value: pltpu.with_memory_space_constraint(value, pltpu.VMEM)

    weights = [
        (to_vmem(value[0, 0]), to_vmem(swap(value[0, 0], "expert", near)))
        for value in (w_gate, w_up, w_down)
    ]
    turned = [jnp.swapaxes(value, 1, 2)[0] for value in (routes, route_gates)]
    tables = list(call(table_body, [full_of(experts, tok_rows)], turned))
    for bit in far_bits:
        tables += [swap(value, "expert", bit) for value in tables]
    (chosen,) = call(
        functools.partial(turn_body, near), [full_of(groups, tok_rows, 8)], tables
    )
    last = [chosen]

    def run(body, outs, ins, **options):
        got = call(body, outs, ins, last[:1], **options)
        last[0] = got[-1]
        return got

    pieces = call(
        split_body,
        [half_of(size, width) for size in sizes],
        [states[0]],
        scratch=[pltpu.SemaphoreType.DMA((len(sizes),))],
        space=pl.BlockSpec(memory_space=pltpu.HBM),
    )

    inward = lambda s: [(s, s + 1), (tracks - 1 - s, tracks - 2 - s)]
    outward = lambda s: [(s, s - 1), (tracks - 1 - s, tracks - s)]
    across = [(middle - 1, middle), (middle, middle - 1)]

    stages = []
    state = [dict() for _ in sizes]
    result = [None]

    def begin(c):
        own = pieces[c]
        state[c]["sum"] = [own]
        state[c]["came"] = lax.ppermute(own, "track", inward(0) if middle > 1 else across)

    def gather(c, step):
        st = state[c]
        st["sum"].append(st["came"])
        (total,) = run(add_body, [half_of(sizes[c], width)], st["sum"])
        if step < middle - 1:
            link = inward(step + 1) if step + 1 < middle - 1 else across
            st["came"] = lax.ppermute(total, "track", link)
        else:
            st["total"] = total
            spread(c, middle - 1)

    def spread(c, step):
        st = state[c]
        if step > 0:
            st["came"] = lax.ppermute(st["total"], "track", outward(step))
        else:
            rows = st["total"]
            parts = [rows]
            for bit in far_bits:
                parts += [swap(value, "expert", bit) for value in parts]
            st["parts"] = parts

    def picked(c, step):
        st = state[c]
        (st["total"],) = run(
            functools.partial(pick_body, step - 1),
            [half_of(sizes[c], width)],
            [st["total"], st["came"]],
        )
        spread(c, step - 1)

    def expert(c):
        st = state[c]
        rows = sizes[c] * groups
        gates, ups, downs = weights

        def body(*refs):
            sources, refs = refs[:groups], refs[groups:]
            expert_body(
                piece, starts[c], sources, refs[0], refs[1], refs[2:4], refs[4:6], refs[6:8], *refs[8:]
            )

        st["keep"], send = run(
            body,
            [full_of(rows, width // 2), half_of(rows, width // 2)],
            [*st["parts"], norm_gain, chosen, *gates, *ups, *downs],
            scratch=[pltpu.VMEM((rows, width), jnp.bfloat16), pltpu.VMEM((rows, 2 * ff), jnp.bfloat16)],
            limit=26,
        )
        st["came"] = swap(send, "track", 1)

    def columns(c, bit):
        st = state[c]
        rows, count = st["keep"].shape
        st["keep"], send = run(
            functools.partial(split_columns_body, bit, piece),
            [full_of(rows, count // 2), half_of(rows, count // 2)],
            [st["keep"], st["came"]],
        )
        st["came"] = swap(send, "track", bit)

    def rows_of(c, bit):
        st = state[c]
        rows, count = st["keep"].shape
        st["keep"], send = run(
            split_rows_body,
            [full_of(rows // 2, count), half_of(rows // 2, count)],
            [st["keep"], st["came"]],
        )
        st["came"] = swap(send, "expert", bit)

    def final(c):
        st = state[c]
        ins = [st["keep"], st["came"], st["total"]]
        others = [other.get("out") for other in state if other is not st]
        if any(other is None for other in others):
            body = functools.partial(final_body, piece, (0,), 0)
            (st["out"],) = run(body, [half_of(sizes[c], piece)], ins)
        else:
            body = functools.partial(final_body, piece, starts, c)
            (result[0],) = run(body, [half_of(tok_rows, piece)], ins + others)

    events = []
    for c in range(len(sizes)):
        wire = starts[c] / tok_rows * WIRE
        own_wire = sizes[c] / tok_rows * WIRE
        hop = HOP + own_wire
        now = wire
        for step in range(middle):
            now += hop
            events.append((now, functools.partial(gather, c, step)))
        for step in range(middle - 1, 0, -1):
            now += hop
            events.append((now, functools.partial(picked, c, step)))
        now += hop * max(1, len(far_bits))
        events.append((now, functools.partial(expert, c)))
        now += EXPERT * sizes[c] / tok_rows
        for bit in bits_of(tracks)[1:]:
            now += hop
            events.append((now, functools.partial(columns, c, bit)))
        now += hop
        for bit in reversed(far_bits):
            events.append((now, functools.partial(rows_of, c, bit)))
            now += HOP + own_wire / 4
        events.append((now, functools.partial(final, c)))
    for c in range(len(sizes)):
        begin(c)
    for _, event in sorted(events, key=lambda item: item[0]):
        event()
    return result[0]


def local(states, routes, route_gates, norm_gain, w_gate, w_up, w_down):
    tok_rows = states.shape[1]
    experts = w_gate.shape[1] * lax.axis_size("expert")
    if 4 * tok_rows // experts < tok_rows or w_gate.shape[1] != 1:
        return dispatched(states, routes, route_gates, norm_gain, w_gate, w_up, w_down)
    return dense(states, routes, route_gates, norm_gain, w_gate, w_up, w_down)


def solution(mesh):
    return jax.shard_map(
        local,
        mesh=mesh,
        in_specs=(
            P("track", ("groups", "expert"), None),
            P("track", ("groups", "expert"), None),
            P("track", ("groups", "expert"), None),
            P("track", None),
            P("track", "expert", None, None),
            P("track", "expert", None, None),
            P("track", "expert", None, None),
        ),
        out_specs=P(("groups", "expert"), "track"),
        check_vma=False,
    )
```

```python
import functools

import jax
import jax.numpy as jnp
from jax import lax
from jax.experimental import pallas as pl
from jax.experimental.pallas import tpu as pltpu
from jax.sharding import PartitionSpec as P

CHUNKS = (1, 1, 1, 1)
HOP, START, WIRE, EXPERT = 1.5, 2.2, 22.5, 12.0
ROWS_FIRST = 2


def slot_places(chosen, experts, capacity):
    flat_ids = chosen.reshape(-1)
    labels = jnp.arange(experts, dtype=jnp.int32)
    matches = (flat_ids[:, None] == labels[None, :]).astype(jnp.int32)
    earlier = jnp.cumsum(matches, axis=0) - matches
    slot_index = jnp.sum(earlier * matches, axis=1)
    return flat_ids * capacity + slot_index


def expert_hidden(arrived, gate_w, up_w, exp_dev):
    sources = arrived.shape[0] // exp_dev
    grouped = arrived.reshape(sources, exp_dev, arrived.shape[1], arrived.shape[2])
    gate_part = jnp.einsum("secd,edf->secf", grouped, gate_w, preferred_element_type=jnp.float32)
    up_part = jnp.einsum("secd,edf->secf", grouped, up_w, preferred_element_type=jnp.float32)
    return (jax.nn.silu(gate_part) * up_part).astype(jnp.bfloat16)


def dispatched(states, routes, route_gates, norm_gain, w_gate, w_up, w_down):
    summed_entry = lax.psum(states[0], "track").astype(jnp.float32)
    tok_rows, model_width = summed_entry.shape
    top_count = routes.shape[2]
    exp_dev = w_gate.shape[1]
    experts = exp_dev * lax.axis_size("expert")
    tracks = lax.axis_size("track")
    capacity = 4 * tok_rows // experts
    slice_width = model_width // tracks
    inverse_rms = lax.rsqrt(jnp.mean(summed_entry * summed_entry, axis=1, keepdims=True) + 1e-06)
    normed = (summed_entry * inverse_rms * norm_gain[0][None, :]).astype(jnp.bfloat16)
    places = slot_places(routes[0], experts, capacity)
    row_owner = jnp.full((experts * capacity,), tok_rows, jnp.int32)
    row_owner = row_owner.at[places].set(
        jnp.arange(top_count * tok_rows, dtype=jnp.int32) // top_count
    )
    outbound = jnp.take(normed, row_owner, axis=0, mode="fill", fill_value=0).reshape(
        experts, capacity, model_width
    )
    own_slice = lax.dynamic_slice_in_dim(
        summed_entry, lax.axis_index("track") * slice_width, slice_width, 1
    )
    arrived = lax.all_to_all(outbound, "expert", split_axis=0, concat_axis=0, tiled=True)
    count_items = arrived.shape[1]
    hidden = expert_hidden(arrived, w_gate[0], w_up[0], exp_dev)
    result = jnp.einsum(
        "secf,efd->secd", hidden, w_down[0], preferred_element_type=jnp.float32
    ).astype(jnp.bfloat16)
    returned = lax.all_to_all(
        result.reshape(experts, count_items, model_width),
        "expert",
        split_axis=0,
        concat_axis=0,
        tiled=True,
    )
    picked = jnp.take(returned.reshape(-1, model_width), places, axis=0)
    branch = jnp.sum(
        picked.reshape(tok_rows, top_count, model_width) * route_gates[0][:, :, None], axis=1
    )
    summed = lax.psum_scatter(
        branch.astype(jnp.bfloat16), "track", scatter_dimension=1, tiled=True
    ).astype(jnp.float32)
    return (own_slice + summed).astype(jnp.bfloat16)


def swap(value, axis, bit):
    size = lax.axis_size(axis)
    return lax.ppermute(value, axis, [(i, i ^ bit) for i in range(size)])


def bits_of(size):
    out, bit = [], 1
    while bit < size:
        out.append(bit)
        bit *= 2
    return out


VMEM = pl.BlockSpec(memory_space=pltpu.VMEM)
ANY = pl.BlockSpec(memory_space=pl.ANY)


def call(body, outs, ins, extra=(), scratch=(), limit=4, space=VMEM):
    count = len(ins)

    def kernel(*refs):
        body(*refs[:count], *refs[count + len(extra) :])

    return pl.pallas_call(
        kernel,
        out_shape=outs,
        in_specs=[space] * len(ins) + [ANY] * len(extra),
        out_specs=[VMEM] * len(outs),
        scratch_shapes=scratch,
        compiler_params=pltpu.CompilerParams(vmem_limit_bytes=limit * 1024 * 1024),
    )(*ins, *extra)


def half_of(*shape):
    return jax.ShapeDtypeStruct(shape, jnp.bfloat16)


def full_of(*shape):
    return jax.ShapeDtypeStruct(shape, jnp.float32)


def add_body(*refs):
    total = refs[0][...].astype(jnp.float32)
    for ref in refs[1:-1]:
        total = total + ref[...].astype(jnp.float32)
    refs[-1][...] = total.astype(jnp.bfloat16)


def pick_body(step, mine, came, out):
    tracks, me = lax.axis_size("track"), lax.axis_index("track")
    takes = (me == step) | (me == tracks - 1 - step)
    out[...] = jnp.where(takes, came[...], mine[...])


def tile_of(size, want):
    while size % want:
        want //= 2
    return want


def table_body(routes, gates, out):
    for expert in range(out.shape[0]):
        named = jnp.where(routes[...] == expert, gates[...], 0.0)
        out[expert : expert + 1] = jnp.sum(named, axis=0, keepdims=True)


def turn_body(near, *refs):
    out = refs[-1]
    me = lax.axis_index("expert")
    for place, ref in enumerate(refs[:-1]):
        table = ref[...]
        rows = table.shape[1]
        labels = lax.broadcasted_iota(jnp.int32, table.shape, 0)
        picked = [
            jnp.sum(jnp.where(labels == named, table, 0.0), axis=0, keepdims=True)
            for named in (me, me ^ near)
        ]
        wide = jnp.concatenate(picked + [jnp.zeros((6, rows), jnp.float32)], axis=0)
        out[place] = jnp.transpose(wide)


def split_body(whole, *refs):
    parts, sems = refs[:-1], refs[-1]
    copies, start = [], 0
    for place, part in enumerate(parts):
        copies.append(
            pltpu.make_async_copy(whole.at[start : start + part.shape[0]], part, sems.at[place])
        )
        copies[-1].start()
        start += part.shape[0]
    for copy in copies:
        copy.wait()


def expert_body(piece, first, sources, gain, weight, gates, ups, downs, keep, send, normed, hidden):
    rows = sources[0].shape[0]
    ff = gates[0].shape[1]
    for place, ref in enumerate(sources):
        wide = ref[...].astype(jnp.float32)
        inverse = lax.rsqrt(jnp.mean(wide * wide, axis=1, keepdims=True) + 1e-06)
        normed[place * rows : (place + 1) * rows] = (wide * inverse * gain[...]).astype(jnp.bfloat16)
    block = tile_of(ff, 256)
    chosen = jnp.concatenate(
        [weight[place, first : first + rows] for place in range(len(sources))], axis=0
    )
    for expert, (gate, up) in enumerate(zip(gates, ups)):

        def hide(step, carry, expert=expert, gate=gate, up=up):
            at = pl.ds(pl.multiple_of(step * block, block), block)
            gate_part = jnp.dot(normed[...], gate[:, at], preferred_element_type=jnp.float32)
            up_part = jnp.dot(normed[...], up[:, at], preferred_element_type=jnp.float32)
            value = jax.nn.silu(gate_part) * up_part * chosen[:, expert : expert + 1]
            to = pl.ds(pl.multiple_of(expert * ff + step * block, block), block)
            hidden[:, to] = value.astype(jnp.bfloat16)
            return carry

        lax.fori_loop(0, ff // block, hide, 0, unroll=True)
    if keep.shape[1] == downs[0].shape[1]:
        half = keep.shape[0]

        def lower_all(step, carry):
            at = pl.ds(pl.multiple_of(step * piece, piece), piece)
            value = jnp.dot(hidden[:, :ff], downs[0][:, at], preferred_element_type=jnp.float32)
            for expert in range(1, len(downs)):
                value += jnp.dot(
                    hidden[:, expert * ff : (expert + 1) * ff],
                    downs[expert][:, at],
                    preferred_element_type=jnp.float32,
                )
            keep[:, at] = value[:half]
            send[:, at] = value[half:].astype(jnp.bfloat16)
            return carry

        lax.fori_loop(0, keep.shape[1] // piece, lower_all, 0, unroll=True)
        return
    parity = lax.axis_index("track") % 2
    for side, out in ((1 - parity, send), (parity, keep)):

        def lower(step, carry, side=side, out=out):
            at = pl.ds(pl.multiple_of((2 * step + side) * piece, piece), piece)
            value = jnp.dot(hidden[:, :ff], downs[0][:, at], preferred_element_type=jnp.float32)
            for expert in range(1, len(downs)):
                value += jnp.dot(
                    hidden[:, expert * ff : (expert + 1) * ff],
                    downs[expert][:, at],
                    preferred_element_type=jnp.float32,
                )
            to = pl.ds(pl.multiple_of(step * piece, piece), piece)
            out[:, to] = value.astype(out.dtype)
            return carry

        lax.fori_loop(0, out.shape[1] // piece, lower, 0, unroll=True)


def split_columns_body(bit, piece, kept, came, keep, send):
    parity = (lax.axis_index("track") // bit) % 2
    for step in range(keep.shape[1] // piece):
        to = slice(step * piece, (step + 1) * piece)
        for side, out in ((1 - parity, send), (parity, keep)):
            at = pl.ds(pl.multiple_of((2 * step + side) * piece, piece), piece)
            out[:, to] = (kept[:, at] + came[:, at].astype(jnp.float32)).astype(out.dtype)


def split_rows_body(kept, came, keep, send):
    rows = keep.shape[0]
    keep[...] = kept[:rows] + came[:rows].astype(jnp.float32)
    send[...] = (kept[rows:] + came[rows:].astype(jnp.float32)).astype(jnp.bfloat16)


def final_body(piece, starts, mine, kept, came, base, *refs):
    out = refs[-1]
    rows = kept.shape[0]
    at = pl.ds(pl.multiple_of(lax.axis_index("track") * piece, piece), piece)
    total = kept[...] + came[...].astype(jnp.float32) + base[:, at].astype(jnp.float32)
    out[starts[mine] : starts[mine] + rows] = total.astype(out.dtype)
    for place, ref in zip((c for c in range(len(starts)) if c != mine), refs[:-1]):
        out[starts[place] : starts[place] + ref.shape[0]] = ref[...]


def order_of(shares, plans, expert):
    free, ready, pending = {}, {}, {}
    now = 0.0

    def launch(c, at):
        link, amount = plans[c][at][1]
        begin = max(now, free.get(link, 0.0))
        free[link] = begin + amount * shares[c] * WIRE
        ready[c] = free[link] + HOP
        pending[c] = at

    def left(c):
        rest = plans[c][pending[c] :]
        return sum(amount * WIRE * shares[c] + HOP + START for _, (_, amount) in rest)

    for c in range(len(shares)):
        launch(c, 0)
    order = []
    while pending:
        now = max(now, min(ready[c] for c in pending))
        c = max((c for c in pending if ready[c] <= now), key=left)
        at = pending.pop(c)
        order.append((c, at))
        now += START + (EXPERT * shares[c] if plans[c][at][0] is expert else 0.1)
        if at + 1 < len(plans[c]):
            launch(c, at + 1)
    return order


def dense(states, routes, route_gates, norm_gain, w_gate, w_up, w_down):
    tok_rows, width = states.shape[1:]
    ff = w_gate.shape[3]
    experts, tracks = lax.axis_size("expert"), lax.axis_size("track")
    middle = tracks // 2
    piece = width // tracks
    far_bits = list(reversed(bits_of(experts)))[:-1]
    near = bits_of(experts)[0]
    groups = 2 ** len(far_bits)

    sizes = [tok_rows * part // sum(CHUNKS) for part in CHUNKS]
    starts = [sum(sizes[:c]) for c in range(len(sizes))]
    to_vmem = lambda value: pltpu.with_memory_space_constraint(value, pltpu.VMEM)

    weights = [
        (to_vmem(value[0, 0]), to_vmem(swap(value[0, 0], "expert", near)))
        for value in (w_gate, w_up, w_down)
    ]
    turned = [jnp.swapaxes(value, 1, 2)[0] for value in (routes, route_gates)]
    tables = list(call(table_body, [full_of(experts, tok_rows)], turned))
    for bit in far_bits:
        tables += [swap(value, "expert", bit) for value in tables]
    (chosen,) = call(
        functools.partial(turn_body, near), [full_of(groups, tok_rows, 8)], tables
    )
    last = [chosen]

    def run(body, outs, ins, **options):
        got = call(body, outs, ins, last[:1], **options)
        last[0] = got[-1]
        return got

    def trade(value, axis, bit):
        return lax.ppermute(value, axis, [(i, i ^ bit) for i in range(lax.axis_size(axis))])

    pieces = call(
        split_body,
        [half_of(size, width) for size in sizes],
        [states[0]],
        scratch=[pltpu.SemaphoreType.DMA((len(sizes),))],
        space=pl.BlockSpec(memory_space=pltpu.HBM),
    )

    inward = lambda s: [(s, s + 1), (tracks - 1 - s, tracks - 2 - s)]
    outward = lambda s: [(s, s - 1), (tracks - 1 - s, tracks - s)]
    across = [(middle - 1, middle), (middle, middle - 1)]

    state = [dict() for _ in sizes]
    result = [None]

    def begin(c):
        own = pieces[c]
        state[c]["sum"] = [own]
        state[c]["came"] = lax.ppermute(own, "track", inward(0) if middle > 1 else across)

    def gather(c, step):
        st = state[c]
        st["sum"].append(st["came"])
        (total,) = run(add_body, [half_of(sizes[c], width)], st["sum"])
        if step < middle - 1:
            link = inward(step + 1) if step + 1 < middle - 1 else across
            st["came"] = lax.ppermute(total, "track", link)
        else:
            st["total"] = total
            spread(c, middle - 1)

    def spread(c, step):
        st = state[c]
        if step > 0:
            st["came"] = lax.ppermute(st["total"], "track", outward(step))
        else:
            rows = st["total"]
            parts = [rows]
            for bit in far_bits:
                parts += [trade(value, "expert", bit) for value in parts]
            st["parts"] = parts

    def picked(c, step):
        st = state[c]
        (st["total"],) = run(
            functools.partial(pick_body, step - 1),
            [half_of(sizes[c], width)],
            [st["total"], st["came"]],
        )
        spread(c, step - 1)

    def expert(c):
        st = state[c]
        rows = sizes[c] * groups
        gates, ups, downs = weights

        def body(*refs):
            sources, refs = refs[:groups], refs[groups:]
            expert_body(
                piece, starts[c], sources, refs[0], refs[1], refs[2:4], refs[4:6], refs[6:8], *refs[8:]
            )

        rows_first = c >= len(sizes) - ROWS_FIRST
        shape = (rows // 2, width) if rows_first else (rows, width // 2)
        st["keep"], send = run(
            body,
            [full_of(*shape), half_of(*shape)],
            [*st["parts"], norm_gain, chosen, *gates, *ups, *downs],
            scratch=[pltpu.VMEM((rows, width), jnp.bfloat16), pltpu.VMEM((rows, 2 * ff), jnp.bfloat16)],
            limit=26,
        )
        if rows_first:
            st["came"] = trade(send, "expert", far_bits[-1])
        else:
            st["came"] = trade(send, "track", 1)

    def columns(c, bit):
        st = state[c]
        rows, count = st["keep"].shape
        st["keep"], send = run(
            functools.partial(split_columns_body, bit, piece),
            [full_of(rows, count // 2), half_of(rows, count // 2)],
            [st["keep"], st["came"]],
        )
        st["came"] = trade(send, "track", bit)

    def rows_of(c, bit):
        st = state[c]
        rows, count = st["keep"].shape
        st["keep"], send = run(
            split_rows_body,
            [full_of(rows // 2, count), half_of(rows // 2, count)],
            [st["keep"], st["came"]],
        )
        st["came"] = trade(send, "expert", bit)

    def final(c):
        st = state[c]
        ins = [st["keep"], st["came"], st["total"]]
        others = [other.get("out") for other in state if other is not st]
        if any(other is None for other in others):
            body = functools.partial(final_body, piece, (0,), 0)
            (st["out"],) = run(body, [half_of(sizes[c], piece)], ins)
        else:
            body = functools.partial(final_body, piece, starts, c)
            (result[0],) = run(body, [half_of(tok_rows, piece)], ins + others)

    steps = [(functools.partial(gather, step=step), ("in", 1.0)) for step in range(middle)]
    steps[-1] = (steps[-1][0], ("mid", 1.0))
    steps += [
        (functools.partial(picked, step=step), ("out", 1.0)) for step in range(middle - 1, 0, -1)
    ]
    steps += [(expert, ("x", 1.0))]

    def tail(rows_first):
        trades = [(rows_of, "x", bit) for bit in reversed(far_bits)]
        trades = [(columns, "z", bit) for bit in bits_of(tracks)] + trades
        if rows_first:
            trades = trades[len(bits_of(tracks)) :] + trades[: len(bits_of(tracks))]
        amount = 1.0 if groups > 1 else 0.5
        out = []
        for (_, link, bit), after in zip(trades, trades[1:] + [None]):
            if link == "z":
                link, load = ("out" if bit == 1 else "mid"), amount * bit
            else:
                load = amount
            amount /= 2
            if after is None:
                step = final
            else:
                step = functools.partial(after[0], bit=after[2])
            out.append((step, (link, load)))
        return out

    plans = []
    for c in range(len(sizes)):
        plans.append(steps + tail(c >= len(sizes) - ROWS_FIRST))
    shares = [size / tok_rows for size in sizes]
    for c in range(len(sizes)):
        begin(c)
    for c, at in order_of(shares, plans, expert):
        plans[c][at][0](c)
    return result[0]


def local(states, routes, route_gates, norm_gain, w_gate, w_up, w_down):
    tok_rows = states.shape[1]
    experts = w_gate.shape[1] * lax.axis_size("expert")
    if 4 * tok_rows // experts < tok_rows or w_gate.shape[1] != 1:
        return dispatched(states, routes, route_gates, norm_gain, w_gate, w_up, w_down)
    return dense(states, routes, route_gates, norm_gain, w_gate, w_up, w_down)


def solution(mesh):
    return jax.shard_map(
        local,
        mesh=mesh,
        in_specs=(
            P("track", ("groups", "expert"), None),
            P("track", ("groups", "expert"), None),
            P("track", ("groups", "expert"), None),
            P("track", None),
            P("track", "expert", None, None),
            P("track", "expert", None, None),
            P("track", "expert", None, None),
        ),
        out_specs=P(("groups", "expert"), "track"),
        check_vma=False,
    )
```

```python
import functools

import jax
import jax.numpy as jnp
from jax import lax
from jax.experimental import pallas as pl
from jax.experimental.pallas import tpu as pltpu
from jax.sharding import PartitionSpec as P

CHUNKS = (1, 1, 1, 1)
HOP, START, MIDDLE, WIRE, EXPERT = 2.5, 2.0, 0.0, 22.5, 16.0
SLACK, OLDEST = 0.0, False
TUNED = ()
ROWS_FIRST = 2


def slot_places(chosen, experts, capacity):
    flat_ids = chosen.reshape(-1)
    labels = jnp.arange(experts, dtype=jnp.int32)
    matches = (flat_ids[:, None] == labels[None, :]).astype(jnp.int32)
    earlier = jnp.cumsum(matches, axis=0) - matches
    slot_index = jnp.sum(earlier * matches, axis=1)
    return flat_ids * capacity + slot_index


def expert_hidden(arrived, gate_w, up_w, exp_dev):
    sources = arrived.shape[0] // exp_dev
    grouped = arrived.reshape(sources, exp_dev, arrived.shape[1], arrived.shape[2])
    gate_part = jnp.einsum("secd,edf->secf", grouped, gate_w, preferred_element_type=jnp.float32)
    up_part = jnp.einsum("secd,edf->secf", grouped, up_w, preferred_element_type=jnp.float32)
    return (jax.nn.silu(gate_part) * up_part).astype(jnp.bfloat16)


def dispatched(states, routes, route_gates, norm_gain, w_gate, w_up, w_down):
    summed_entry = lax.psum(states[0], "track").astype(jnp.float32)
    tok_rows, model_width = summed_entry.shape
    top_count = routes.shape[2]
    exp_dev = w_gate.shape[1]
    experts = exp_dev * lax.axis_size("expert")
    tracks = lax.axis_size("track")
    capacity = 4 * tok_rows // experts
    slice_width = model_width // tracks
    inverse_rms = lax.rsqrt(jnp.mean(summed_entry * summed_entry, axis=1, keepdims=True) + 1e-06)
    normed = (summed_entry * inverse_rms * norm_gain[0][None, :]).astype(jnp.bfloat16)
    places = slot_places(routes[0], experts, capacity)
    row_owner = jnp.full((experts * capacity,), tok_rows, jnp.int32)
    row_owner = row_owner.at[places].set(
        jnp.arange(top_count * tok_rows, dtype=jnp.int32) // top_count
    )
    outbound = jnp.take(normed, row_owner, axis=0, mode="fill", fill_value=0).reshape(
        experts, capacity, model_width
    )
    own_slice = lax.dynamic_slice_in_dim(
        summed_entry, lax.axis_index("track") * slice_width, slice_width, 1
    )
    arrived = lax.all_to_all(outbound, "expert", split_axis=0, concat_axis=0, tiled=True)
    count_items = arrived.shape[1]
    hidden = expert_hidden(arrived, w_gate[0], w_up[0], exp_dev)
    result = jnp.einsum(
        "secf,efd->secd", hidden, w_down[0], preferred_element_type=jnp.float32
    ).astype(jnp.bfloat16)
    returned = lax.all_to_all(
        result.reshape(experts, count_items, model_width),
        "expert",
        split_axis=0,
        concat_axis=0,
        tiled=True,
    )
    picked = jnp.take(returned.reshape(-1, model_width), places, axis=0)
    branch = jnp.sum(
        picked.reshape(tok_rows, top_count, model_width) * route_gates[0][:, :, None], axis=1
    )
    summed = lax.psum_scatter(
        branch.astype(jnp.bfloat16), "track", scatter_dimension=1, tiled=True
    ).astype(jnp.float32)
    return (own_slice + summed).astype(jnp.bfloat16)


def swap(value, axis, bit):
    size = lax.axis_size(axis)
    return lax.ppermute(value, axis, [(i, i ^ bit) for i in range(size)])


def bits_of(size):
    out, bit = [], 1
    while bit < size:
        out.append(bit)
        bit *= 2
    return out


VMEM = pl.BlockSpec(memory_space=pltpu.VMEM)
ANY = pl.BlockSpec(memory_space=pl.ANY)


def call(body, outs, ins, extra=(), scratch=(), limit=4, space=VMEM):
    count = len(ins)

    def kernel(*refs):
        body(*refs[:count], *refs[count + len(extra) :])

    return pl.pallas_call(
        kernel,
        out_shape=outs,
        in_specs=[space] * len(ins) + [ANY] * len(extra),
        out_specs=[VMEM] * len(outs),
        scratch_shapes=scratch,
        compiler_params=pltpu.CompilerParams(vmem_limit_bytes=limit * 1024 * 1024),
    )(*ins, *extra)


def half_of(*shape):
    return jax.ShapeDtypeStruct(shape, jnp.bfloat16)


def full_of(*shape):
    return jax.ShapeDtypeStruct(shape, jnp.float32)


def add_body(*refs):
    total = refs[0][...].astype(jnp.float32)
    for ref in refs[1:-1]:
        total = total + ref[...].astype(jnp.float32)
    refs[-1][...] = total.astype(jnp.bfloat16)


def pick_body(step, mine, came, out):
    tracks, me = lax.axis_size("track"), lax.axis_index("track")
    takes = (me == step) | (me == tracks - 1 - step)
    out[...] = jnp.where(takes, came[...], mine[...])


def tile_of(size, want):
    while size % want:
        want //= 2
    return want


def table_body(routes, gates, out):
    for expert in range(out.shape[0]):
        named = jnp.where(routes[...] == expert, gates[...], 0.0)
        out[expert : expert + 1] = jnp.sum(named, axis=0, keepdims=True)


def turn_body(near, *refs):
    out = refs[-1]
    me = lax.axis_index("expert")
    for place, ref in enumerate(refs[:-1]):
        table = ref[...]
        rows = table.shape[1]
        labels = lax.broadcasted_iota(jnp.int32, table.shape, 0)
        picked = [
            jnp.sum(jnp.where(labels == named, table, 0.0), axis=0, keepdims=True)
            for named in (me, me ^ near)
        ]
        wide = jnp.concatenate(picked + [jnp.zeros((6, rows), jnp.float32)], axis=0)
        out[place] = jnp.transpose(wide)


def split_body(whole, *refs):
    parts, sems = refs[:-1], refs[-1]
    copies, start = [], 0
    for place, part in enumerate(parts):
        copies.append(
            pltpu.make_async_copy(whole.at[start : start + part.shape[0]], part, sems.at[place])
        )
        copies[-1].start()
        start += part.shape[0]
    for copy in copies:
        copy.wait()


def expert_body(piece, first, sources, gain, weight, gates, ups, downs, keep, send, normed, hidden):
    rows = sources[0].shape[0]
    ff = gates[0].shape[1]
    for place, ref in enumerate(sources):
        wide = ref[...].astype(jnp.float32)
        inverse = lax.rsqrt(jnp.mean(wide * wide, axis=1, keepdims=True) + 1e-06)
        normed[place * rows : (place + 1) * rows] = (wide * inverse * gain[...]).astype(jnp.bfloat16)
    block = tile_of(ff, 256)
    chosen = jnp.concatenate(
        [weight[place, first : first + rows] for place in range(len(sources))], axis=0
    )
    for expert, (gate, up) in enumerate(zip(gates, ups)):

        def hide(step, carry, expert=expert, gate=gate, up=up):
            at = pl.ds(pl.multiple_of(step * block, block), block)
            gate_part = jnp.dot(normed[...], gate[:, at], preferred_element_type=jnp.float32)
            up_part = jnp.dot(normed[...], up[:, at], preferred_element_type=jnp.float32)
            value = jax.nn.silu(gate_part) * up_part * chosen[:, expert : expert + 1]
            to = pl.ds(pl.multiple_of(expert * ff + step * block, block), block)
            hidden[:, to] = value.astype(jnp.bfloat16)
            return carry

        lax.fori_loop(0, ff // block, hide, 0, unroll=True)
    if keep.shape[1] == downs[0].shape[1]:
        half = keep.shape[0]

        def lower_all(step, carry):
            at = pl.ds(pl.multiple_of(step * piece, piece), piece)
            value = jnp.dot(hidden[:, :ff], downs[0][:, at], preferred_element_type=jnp.float32)
            for expert in range(1, len(downs)):
                value += jnp.dot(
                    hidden[:, expert * ff : (expert + 1) * ff],
                    downs[expert][:, at],
                    preferred_element_type=jnp.float32,
                )
            keep[:, at] = value[:half]
            send[:, at] = value[half:].astype(jnp.bfloat16)
            return carry

        lax.fori_loop(0, keep.shape[1] // piece, lower_all, 0, unroll=True)
        return
    parity = lax.axis_index("track") % 2
    for side, out in ((1 - parity, send), (parity, keep)):

        def lower(step, carry, side=side, out=out):
            at = pl.ds(pl.multiple_of((2 * step + side) * piece, piece), piece)
            value = jnp.dot(hidden[:, :ff], downs[0][:, at], preferred_element_type=jnp.float32)
            for expert in range(1, len(downs)):
                value += jnp.dot(
                    hidden[:, expert * ff : (expert + 1) * ff],
                    downs[expert][:, at],
                    preferred_element_type=jnp.float32,
                )
            to = pl.ds(pl.multiple_of(step * piece, piece), piece)
            out[:, to] = value.astype(out.dtype)
            return carry

        lax.fori_loop(0, out.shape[1] // piece, lower, 0, unroll=True)


def split_columns_body(bit, piece, kept, came, keep, send):
    parity = (lax.axis_index("track") // bit) % 2
    for step in range(keep.shape[1] // piece):
        to = slice(step * piece, (step + 1) * piece)
        for side, out in ((1 - parity, send), (parity, keep)):
            at = pl.ds(pl.multiple_of((2 * step + side) * piece, piece), piece)
            out[:, to] = (kept[:, at] + came[:, at].astype(jnp.float32)).astype(out.dtype)


def split_rows_body(kept, came, keep, send):
    rows = keep.shape[0]
    keep[...] = kept[:rows] + came[:rows].astype(jnp.float32)
    send[...] = (kept[rows:] + came[rows:].astype(jnp.float32)).astype(jnp.bfloat16)


def final_body(piece, starts, mine, kept, came, base, *refs):
    out = refs[-1]
    rows = kept.shape[0]
    at = pl.ds(pl.multiple_of(lax.axis_index("track") * piece, piece), piece)
    total = kept[...] + came[...].astype(jnp.float32) + base[:, at].astype(jnp.float32)
    out[starts[mine] : starts[mine] + rows] = total.astype(out.dtype)
    for place, ref in zip((c for c in range(len(starts)) if c != mine), refs[:-1]):
        out[starts[place] : starts[place] + ref.shape[0]] = ref[...]


def order_of(shares, plans, expert):
    free, ready, pending = {}, {}, {}
    now = 0.0

    def launch(c, at):
        link, amount = plans[c][at][1]
        begin = max(now, free.get(link, 0.0))
        free[link] = begin + amount * shares[c] * WIRE
        ready[c] = free[link] + HOP
        pending[c] = at

    def left(c):
        rest = plans[c][pending[c] :]
        return sum(amount * WIRE * shares[c] + HOP + START for _, (_, amount) in rest)

    for c in range(len(shares)):
        launch(c, 0)
    order = []
    while pending:
        now = max(now, min(ready[c] for c in pending))
        able = [c for c in pending if ready[c] <= now + SLACK]
        c = min(able) if OLDEST else max(able, key=left)
        now = max(now, ready[c])
        at = pending.pop(c)
        order.append((c, at))
        now += EXPERT * shares[c] if plans[c][at][0] is expert else 0.1
        if at + 1 < len(plans[c]):
            now += START + (MIDDLE if plans[c][at + 1][1][0] == "mid" else 0.0)
            launch(c, at + 1)
    return order


def dense(states, routes, route_gates, norm_gain, w_gate, w_up, w_down):
    tok_rows, width = states.shape[1:]
    ff = w_gate.shape[3]
    experts, tracks = lax.axis_size("expert"), lax.axis_size("track")
    middle = tracks // 2
    piece = width // tracks
    far_bits = list(reversed(bits_of(experts)))[:-1]
    near = bits_of(experts)[0]
    groups = 2 ** len(far_bits)

    sizes = [tok_rows * part // sum(CHUNKS) for part in CHUNKS]
    starts = [sum(sizes[:c]) for c in range(len(sizes))]
    to_vmem = lambda value: pltpu.with_memory_space_constraint(value, pltpu.VMEM)

    weights = [
        (to_vmem(value[0, 0]), to_vmem(swap(value[0, 0], "expert", near)))
        for value in (w_gate, w_up, w_down)
    ]
    turned = [jnp.swapaxes(value, 1, 2)[0] for value in (routes, route_gates)]
    tables = list(call(table_body, [full_of(experts, tok_rows)], turned))
    for bit in far_bits:
        tables += [swap(value, "expert", bit) for value in tables]
    (chosen,) = call(
        functools.partial(turn_body, near), [full_of(groups, tok_rows, 8)], tables
    )
    last = [chosen]

    def run(body, outs, ins, **options):
        got = call(body, outs, ins, last[:1], **options)
        last[0] = got[-1]
        return got

    def trade(value, axis, bit):
        return lax.ppermute(value, axis, [(i, i ^ bit) for i in range(lax.axis_size(axis))])

    pieces = call(
        split_body,
        [half_of(size, width) for size in sizes],
        [states[0]],
        scratch=[pltpu.SemaphoreType.DMA((len(sizes),))],
        space=pl.BlockSpec(memory_space=pltpu.HBM),
    )

    inward = lambda s: [(s, s + 1), (tracks - 1 - s, tracks - 2 - s)]
    outward = lambda s: [(s, s - 1), (tracks - 1 - s, tracks - s)]
    across = [(middle - 1, middle), (middle, middle - 1)]

    state = [dict() for _ in sizes]
    result = [None]

    def begin(c):
        own = pieces[c]
        state[c]["sum"] = [own]
        state[c]["came"] = lax.ppermute(own, "track", inward(0) if middle > 1 else across)

    def gather(c, step):
        st = state[c]
        st["sum"].append(st["came"])
        (total,) = run(add_body, [half_of(sizes[c], width)], st["sum"])
        if step < middle - 1:
            link = inward(step + 1) if step + 1 < middle - 1 else across
            st["came"] = lax.ppermute(total, "track", link)
        else:
            st["total"] = total
            spread(c, middle - 1)

    def spread(c, step):
        st = state[c]
        if step > 0:
            st["came"] = lax.ppermute(st["total"], "track", outward(step))
        else:
            rows = st["total"]
            parts = [rows]
            for bit in far_bits:
                parts += [trade(value, "expert", bit) for value in parts]
            st["parts"] = parts

    def picked(c, step):
        st = state[c]
        (st["total"],) = run(
            functools.partial(pick_body, step - 1),
            [half_of(sizes[c], width)],
            [st["total"], st["came"]],
        )
        spread(c, step - 1)

    def expert(c):
        st = state[c]
        rows = sizes[c] * groups
        gates, ups, downs = weights

        def body(*refs):
            sources, refs = refs[:groups], refs[groups:]
            expert_body(
                piece, starts[c], sources, refs[0], refs[1], refs[2:4], refs[4:6], refs[6:8], *refs[8:]
            )

        rows_first = c >= len(sizes) - ROWS_FIRST
        shape = (rows // 2, width) if rows_first else (rows, width // 2)
        st["keep"], send = run(
            body,
            [full_of(*shape), half_of(*shape)],
            [*st["parts"], norm_gain, chosen, *gates, *ups, *downs],
            scratch=[pltpu.VMEM((rows, width), jnp.bfloat16), pltpu.VMEM((rows, 2 * ff), jnp.bfloat16)],
            limit=26,
        )
        if rows_first:
            st["came"] = trade(send, "expert", far_bits[-1])
        else:
            st["came"] = trade(send, "track", 1)

    def columns(c, bit):
        st = state[c]
        rows, count = st["keep"].shape
        st["keep"], send = run(
            functools.partial(split_columns_body, bit, piece),
            [full_of(rows, count // 2), half_of(rows, count // 2)],
            [st["keep"], st["came"]],
        )
        st["came"] = trade(send, "track", bit)

    def rows_of(c, bit):
        st = state[c]
        rows, count = st["keep"].shape
        st["keep"], send = run(
            split_rows_body,
            [full_of(rows // 2, count), half_of(rows // 2, count)],
            [st["keep"], st["came"]],
        )
        st["came"] = trade(send, "expert", bit)

    def final(c):
        st = state[c]
        ins = [st["keep"], st["came"], st["total"]]
        others = [other.get("out") for other in state if other is not st]
        if any(other is None for other in others):
            body = functools.partial(final_body, piece, (0,), 0)
            (st["out"],) = run(body, [half_of(sizes[c], piece)], ins)
        else:
            body = functools.partial(final_body, piece, starts, c)
            (result[0],) = run(body, [half_of(tok_rows, piece)], ins + others)

    steps = [(functools.partial(gather, step=step), ("in", 1.0)) for step in range(middle)]
    steps[-1] = (steps[-1][0], ("mid", 1.0))
    steps += [
        (functools.partial(picked, step=step), ("out", 1.0)) for step in range(middle - 1, 0, -1)
    ]
    steps += [(expert, ("x", 1.0))]

    def tail(rows_first):
        trades = [(rows_of, "x", bit) for bit in reversed(far_bits)]
        trades = [(columns, "z", bit) for bit in bits_of(tracks)] + trades
        if rows_first:
            trades = trades[len(bits_of(tracks)) :] + trades[: len(bits_of(tracks))]
        amount = 1.0 if groups > 1 else 0.5
        out = []
        for (_, link, bit), after in zip(trades, trades[1:] + [None]):
            if link == "z":
                link, load = ("out" if bit == 1 else "mid"), amount * bit
            else:
                load = amount
            amount /= 2
            if after is None:
                step = final
            else:
                step = functools.partial(after[0], bit=after[2])
            out.append((step, (link, load)))
        return out

    plans = []
    for c in range(len(sizes)):
        plans.append(steps + tail(c >= len(sizes) - ROWS_FIRST))
    shares = [size / tok_rows for size in sizes]
    for c in range(len(sizes)):
        begin(c)
    order = order_of(shares, plans, expert)
    if sorted(order) == sorted(TUNED):
        order = TUNED
    for c, at in order:
        plans[c][at][0](c)
    return result[0]


def local(states, routes, route_gates, norm_gain, w_gate, w_up, w_down):
    tok_rows = states.shape[1]
    experts = w_gate.shape[1] * lax.axis_size("expert")
    if 4 * tok_rows // experts < tok_rows or w_gate.shape[1] != 1:
        return dispatched(states, routes, route_gates, norm_gain, w_gate, w_up, w_down)
    return dense(states, routes, route_gates, norm_gain, w_gate, w_up, w_down)


def solution(mesh):
    return jax.shard_map(
        local,
        mesh=mesh,
        in_specs=(
            P("track", ("groups", "expert"), None),
            P("track", ("groups", "expert"), None),
            P("track", ("groups", "expert"), None),
            P("track", None),
            P("track", "expert", None, None),
            P("track", "expert", None, None),
            P("track", "expert", None, None),
        ),
        out_specs=P(("groups", "expert"), "track"),
        check_vma=False,
    )
```

```python
import functools

import jax
import jax.numpy as jnp
from jax import lax
from jax.experimental import pallas as pl
from jax.experimental.pallas import tpu as pltpu
from jax.sharding import PartitionSpec as P

CHUNKS = (1, 1, 1, 1)
HOP, START, MIDDLE, WIRE, EXPERT = 2.5, 2.0, 0.0, 22.5, 16.0
SLACK, OLDEST = 0.0, False
TUNED = ((0, 0), (1, 0), (0, 1), (2, 0), (1, 1), (0, 2), (3, 0), (2, 1), (1, 2), (3, 1), (0, 3), (2, 2), (3, 2), (1, 3), (0, 4), (2, 3), (3, 3), (1, 4), (0, 5), (2, 4), (3, 4), (1, 5), (2, 5), (0, 6), (3, 5), (1, 6), (2, 6), (3, 6))
ROWS_FIRST = 2


def slot_places(chosen, experts, capacity):
    flat_ids = chosen.reshape(-1)
    labels = jnp.arange(experts, dtype=jnp.int32)
    matches = (flat_ids[:, None] == labels[None, :]).astype(jnp.int32)
    earlier = jnp.cumsum(matches, axis=0) - matches
    slot_index = jnp.sum(earlier * matches, axis=1)
    return flat_ids * capacity + slot_index


def expert_hidden(arrived, gate_w, up_w, exp_dev):
    sources = arrived.shape[0] // exp_dev
    grouped = arrived.reshape(sources, exp_dev, arrived.shape[1], arrived.shape[2])
    gate_part = jnp.einsum("secd,edf->secf", grouped, gate_w, preferred_element_type=jnp.float32)
    up_part = jnp.einsum("secd,edf->secf", grouped, up_w, preferred_element_type=jnp.float32)
    return (jax.nn.silu(gate_part) * up_part).astype(jnp.bfloat16)


def dispatched(states, routes, route_gates, norm_gain, w_gate, w_up, w_down):
    summed_entry = lax.psum(states[0], "track").astype(jnp.float32)
    tok_rows, model_width = summed_entry.shape
    top_count = routes.shape[2]
    exp_dev = w_gate.shape[1]
    experts = exp_dev * lax.axis_size("expert")
    tracks = lax.axis_size("track")
    capacity = 4 * tok_rows // experts
    slice_width = model_width // tracks
    inverse_rms = lax.rsqrt(jnp.mean(summed_entry * summed_entry, axis=1, keepdims=True) + 1e-06)
    normed = (summed_entry * inverse_rms * norm_gain[0][None, :]).astype(jnp.bfloat16)
    places = slot_places(routes[0], experts, capacity)
    row_owner = jnp.full((experts * capacity,), tok_rows, jnp.int32)
    row_owner = row_owner.at[places].set(
        jnp.arange(top_count * tok_rows, dtype=jnp.int32) // top_count
    )
    outbound = jnp.take(normed, row_owner, axis=0, mode="fill", fill_value=0).reshape(
        experts, capacity, model_width
    )
    own_slice = lax.dynamic_slice_in_dim(
        summed_entry, lax.axis_index("track") * slice_width, slice_width, 1
    )
    arrived = lax.all_to_all(outbound, "expert", split_axis=0, concat_axis=0, tiled=True)
    count_items = arrived.shape[1]
    hidden = expert_hidden(arrived, w_gate[0], w_up[0], exp_dev)
    result = jnp.einsum(
        "secf,efd->secd", hidden, w_down[0], preferred_element_type=jnp.float32
    ).astype(jnp.bfloat16)
    returned = lax.all_to_all(
        result.reshape(experts, count_items, model_width),
        "expert",
        split_axis=0,
        concat_axis=0,
        tiled=True,
    )
    picked = jnp.take(returned.reshape(-1, model_width), places, axis=0)
    branch = jnp.sum(
        picked.reshape(tok_rows, top_count, model_width) * route_gates[0][:, :, None], axis=1
    )
    summed = lax.psum_scatter(
        branch.astype(jnp.bfloat16), "track", scatter_dimension=1, tiled=True
    ).astype(jnp.float32)
    return (own_slice + summed).astype(jnp.bfloat16)


def swap(value, axis, bit):
    size = lax.axis_size(axis)
    return lax.ppermute(value, axis, [(i, i ^ bit) for i in range(size)])


def bits_of(size):
    out, bit = [], 1
    while bit < size:
        out.append(bit)
        bit *= 2
    return out


VMEM = pl.BlockSpec(memory_space=pltpu.VMEM)
ANY = pl.BlockSpec(memory_space=pl.ANY)


def call(body, outs, ins, extra=(), scratch=(), limit=4, space=VMEM):
    count = len(ins)

    def kernel(*refs):
        body(*refs[:count], *refs[count + len(extra) :])

    return pl.pallas_call(
        kernel,
        out_shape=outs,
        in_specs=[space] * len(ins) + [ANY] * len(extra),
        out_specs=[VMEM] * len(outs),
        scratch_shapes=scratch,
        compiler_params=pltpu.CompilerParams(vmem_limit_bytes=limit * 1024 * 1024),
    )(*ins, *extra)


def half_of(*shape):
    return jax.ShapeDtypeStruct(shape, jnp.bfloat16)


def full_of(*shape):
    return jax.ShapeDtypeStruct(shape, jnp.float32)


def add_body(*refs):
    total = refs[0][...].astype(jnp.float32)
    for ref in refs[1:-1]:
        total = total + ref[...].astype(jnp.float32)
    refs[-1][...] = total.astype(jnp.bfloat16)


def pick_body(step, mine, came, out):
    tracks, me = lax.axis_size("track"), lax.axis_index("track")
    takes = (me == step) | (me == tracks - 1 - step)
    out[...] = jnp.where(takes, came[...], mine[...])


def tile_of(size, want):
    while size % want:
        want //= 2
    return want


def table_body(routes, gates, out):
    for expert in range(out.shape[0]):
        named = jnp.where(routes[...] == expert, gates[...], 0.0)
        out[expert : expert + 1] = jnp.sum(named, axis=0, keepdims=True)


def turn_body(near, *refs):
    out = refs[-1]
    me = lax.axis_index("expert")
    for place, ref in enumerate(refs[:-1]):
        table = ref[...]
        rows = table.shape[1]
        labels = lax.broadcasted_iota(jnp.int32, table.shape, 0)
        picked = [
            jnp.sum(jnp.where(labels == named, table, 0.0), axis=0, keepdims=True)
            for named in (me, me ^ near)
        ]
        wide = jnp.concatenate(picked + [jnp.zeros((6, rows), jnp.float32)], axis=0)
        out[place] = jnp.transpose(wide)


def split_body(whole, *refs):
    parts, sems = refs[:-1], refs[-1]
    copies, start = [], 0
    for place, part in enumerate(parts):
        copies.append(
            pltpu.make_async_copy(whole.at[start : start + part.shape[0]], part, sems.at[place])
        )
        copies[-1].start()
        start += part.shape[0]
    for copy in copies:
        copy.wait()


def expert_body(piece, first, sources, gain, weight, gates, ups, downs, keep, send, normed, hidden):
    rows = sources[0].shape[0]
    ff = gates[0].shape[1]
    for place, ref in enumerate(sources):
        wide = ref[...].astype(jnp.float32)
        inverse = lax.rsqrt(jnp.mean(wide * wide, axis=1, keepdims=True) + 1e-06)
        normed[place * rows : (place + 1) * rows] = (wide * inverse * gain[...]).astype(jnp.bfloat16)
    block = tile_of(ff, 256)
    chosen = jnp.concatenate(
        [weight[place, first : first + rows] for place in range(len(sources))], axis=0
    )
    for expert, (gate, up) in enumerate(zip(gates, ups)):

        def hide(step, carry, expert=expert, gate=gate, up=up):
            at = pl.ds(pl.multiple_of(step * block, block), block)
            gate_part = jnp.dot(normed[...], gate[:, at], preferred_element_type=jnp.float32)
            up_part = jnp.dot(normed[...], up[:, at], preferred_element_type=jnp.float32)
            value = jax.nn.silu(gate_part) * up_part * chosen[:, expert : expert + 1]
            to = pl.ds(pl.multiple_of(expert * ff + step * block, block), block)
            hidden[:, to] = value.astype(jnp.bfloat16)
            return carry

        lax.fori_loop(0, ff // block, hide, 0, unroll=True)
    if keep.shape[1] == downs[0].shape[1]:
        half = keep.shape[0]

        def lower_all(step, carry):
            at = pl.ds(pl.multiple_of(step * piece, piece), piece)
            value = jnp.dot(hidden[:, :ff], downs[0][:, at], preferred_element_type=jnp.float32)
            for expert in range(1, len(downs)):
                value += jnp.dot(
                    hidden[:, expert * ff : (expert + 1) * ff],
                    downs[expert][:, at],
                    preferred_element_type=jnp.float32,
                )
            keep[:, at] = value[:half]
            send[:, at] = value[half:].astype(jnp.bfloat16)
            return carry

        lax.fori_loop(0, keep.shape[1] // piece, lower_all, 0, unroll=True)
        return
    parity = lax.axis_index("track") % 2
    for side, out in ((1 - parity, send), (parity, keep)):

        def lower(step, carry, side=side, out=out):
            at = pl.ds(pl.multiple_of((2 * step + side) * piece, piece), piece)
            value = jnp.dot(hidden[:, :ff], downs[0][:, at], preferred_element_type=jnp.float32)
            for expert in range(1, len(downs)):
                value += jnp.dot(
                    hidden[:, expert * ff : (expert + 1) * ff],
                    downs[expert][:, at],
                    preferred_element_type=jnp.float32,
                )
            to = pl.ds(pl.multiple_of(step * piece, piece), piece)
            out[:, to] = value.astype(out.dtype)
            return carry

        lax.fori_loop(0, out.shape[1] // piece, lower, 0, unroll=True)


def split_columns_body(bit, piece, kept, came, keep, send):
    parity = (lax.axis_index("track") // bit) % 2
    for step in range(keep.shape[1] // piece):
        to = slice(step * piece, (step + 1) * piece)
        for side, out in ((1 - parity, send), (parity, keep)):
            at = pl.ds(pl.multiple_of((2 * step + side) * piece, piece), piece)
            out[:, to] = (kept[:, at] + came[:, at].astype(jnp.float32)).astype(out.dtype)


def split_rows_body(kept, came, keep, send):
    rows = keep.shape[0]
    keep[...] = kept[:rows] + came[:rows].astype(jnp.float32)
    send[...] = (kept[rows:] + came[rows:].astype(jnp.float32)).astype(jnp.bfloat16)


def final_body(piece, starts, mine, kept, came, base, *refs):
    out = refs[-1]
    rows = kept.shape[0]
    at = pl.ds(pl.multiple_of(lax.axis_index("track") * piece, piece), piece)
    total = kept[...] + came[...].astype(jnp.float32) + base[:, at].astype(jnp.float32)
    out[starts[mine] : starts[mine] + rows] = total.astype(out.dtype)
    for place, ref in zip((c for c in range(len(starts)) if c != mine), refs[:-1]):
        out[starts[place] : starts[place] + ref.shape[0]] = ref[...]


def order_of(shares, plans, expert):
    free, ready, pending = {}, {}, {}
    now = 0.0

    def launch(c, at):
        link, amount = plans[c][at][1]
        begin = max(now, free.get(link, 0.0))
        free[link] = begin + amount * shares[c] * WIRE
        ready[c] = free[link] + HOP
        pending[c] = at

    def left(c):
        rest = plans[c][pending[c] :]
        return sum(amount * WIRE * shares[c] + HOP + START for _, (_, amount) in rest)

    for c in range(len(shares)):
        launch(c, 0)
    order = []
    while pending:
        now = max(now, min(ready[c] for c in pending))
        able = [c for c in pending if ready[c] <= now + SLACK]
        c = min(able) if OLDEST else max(able, key=left)
        now = max(now, ready[c])
        at = pending.pop(c)
        order.append((c, at))
        now += EXPERT * shares[c] if plans[c][at][0] is expert else 0.1
        if at + 1 < len(plans[c]):
            now += START + (MIDDLE if plans[c][at + 1][1][0] == "mid" else 0.0)
            launch(c, at + 1)
    return order


def dense(states, routes, route_gates, norm_gain, w_gate, w_up, w_down):
    tok_rows, width = states.shape[1:]
    ff = w_gate.shape[3]
    experts, tracks = lax.axis_size("expert"), lax.axis_size("track")
    middle = tracks // 2
    piece = width // tracks
    far_bits = list(reversed(bits_of(experts)))[:-1]
    near = bits_of(experts)[0]
    groups = 2 ** len(far_bits)

    sizes = [tok_rows * part // sum(CHUNKS) for part in CHUNKS]
    starts = [sum(sizes[:c]) for c in range(len(sizes))]
    to_vmem = lambda value: pltpu.with_memory_space_constraint(value, pltpu.VMEM)

    weights = []
    for value in (w_gate, w_up, w_down):
        other = swap(value[0, 0], "expert", near)
        weights.append((to_vmem(value[0, 0]), to_vmem(other)))
    turned = [jnp.swapaxes(value, 1, 2)[0] for value in (routes, route_gates)]
    tables = list(call(table_body, [full_of(experts, tok_rows)], turned))
    for bit in far_bits:
        tables += [swap(value, "expert", bit) for value in tables]
    (chosen,) = call(
        functools.partial(turn_body, near), [full_of(groups, tok_rows, 8)], tables
    )
    last = [chosen]

    def run(body, outs, ins, **options):
        got = call(body, outs, ins, last[:1], **options)
        last[0] = got[-1]
        return got

    def trade(value, axis, bit):
        return lax.ppermute(value, axis, [(i, i ^ bit) for i in range(lax.axis_size(axis))])

    pieces = call(
        split_body,
        [half_of(size, width) for size in sizes],
        [states[0]],
        scratch=[pltpu.SemaphoreType.DMA((len(sizes),))],
        space=pl.BlockSpec(memory_space=pltpu.HBM),
    )

    inward = lambda s: [(s, s + 1), (tracks - 1 - s, tracks - 2 - s)]
    outward = lambda s: [(s, s - 1), (tracks - 1 - s, tracks - s)]
    across = [(middle - 1, middle), (middle, middle - 1)]

    state = [dict() for _ in sizes]
    result = [None]

    def begin(c):
        own = pieces[c]
        state[c]["sum"] = [own]
        state[c]["came"] = lax.ppermute(own, "track", inward(0) if middle > 1 else across)

    def gather(c, step):
        st = state[c]
        st["sum"].append(st["came"])
        (total,) = run(add_body, [half_of(sizes[c], width)], st["sum"])
        if step < middle - 1:
            link = inward(step + 1) if step + 1 < middle - 1 else across
            st["came"] = lax.ppermute(total, "track", link)
        else:
            st["total"] = total
            spread(c, middle - 1)

    def spread(c, step):
        st = state[c]
        if step > 0:
            st["came"] = lax.ppermute(st["total"], "track", outward(step))
        else:
            rows = st["total"]
            parts = [rows]
            for bit in far_bits:
                parts += [trade(value, "expert", bit) for value in parts]
            st["parts"] = parts

    def picked(c, step):
        st = state[c]
        (st["total"],) = run(
            functools.partial(pick_body, step - 1),
            [half_of(sizes[c], width)],
            [st["total"], st["came"]],
        )
        spread(c, step - 1)

    def expert(c):
        st = state[c]
        rows = sizes[c] * groups
        gates, ups, downs = weights

        def body(*refs):
            sources, refs = refs[:groups], refs[groups:]
            expert_body(
                piece, starts[c], sources, refs[0], refs[1], refs[2:4], refs[4:6], refs[6:8], *refs[8:]
            )

        rows_first = c >= len(sizes) - ROWS_FIRST
        shape = (rows // 2, width) if rows_first else (rows, width // 2)
        st["keep"], send = run(
            body,
            [full_of(*shape), half_of(*shape)],
            [*st["parts"], norm_gain, chosen, *gates, *ups, *downs],
            scratch=[pltpu.VMEM((rows, width), jnp.bfloat16), pltpu.VMEM((rows, 2 * ff), jnp.bfloat16)],
            limit=26,
        )
        if rows_first:
            st["came"] = trade(send, "expert", far_bits[-1])
        else:
            st["came"] = trade(send, "track", 1)

    def columns(c, bit):
        st = state[c]
        rows, count = st["keep"].shape
        st["keep"], send = run(
            functools.partial(split_columns_body, bit, piece),
            [full_of(rows, count // 2), half_of(rows, count // 2)],
            [st["keep"], st["came"]],
        )
        st["came"] = trade(send, "track", bit)

    def rows_of(c, bit):
        st = state[c]
        rows, count = st["keep"].shape
        st["keep"], send = run(
            split_rows_body,
            [full_of(rows // 2, count), half_of(rows // 2, count)],
            [st["keep"], st["came"]],
        )
        st["came"] = trade(send, "expert", bit)

    def final(c):
        st = state[c]
        ins = [st["keep"], st["came"], st["total"]]
        others = [other.get("out") for other in state if other is not st]
        if any(other is None for other in others):
            body = functools.partial(final_body, piece, (0,), 0)
            (st["out"],) = run(body, [half_of(sizes[c], piece)], ins)
        else:
            body = functools.partial(final_body, piece, starts, c)
            (result[0],) = run(body, [half_of(tok_rows, piece)], ins + others)

    steps = [(functools.partial(gather, step=step), ("in", 1.0)) for step in range(middle)]
    steps[-1] = (steps[-1][0], ("mid", 1.0))
    steps += [
        (functools.partial(picked, step=step), ("out", 1.0)) for step in range(middle - 1, 0, -1)
    ]
    steps += [(expert, ("x", 1.0))]

    def tail(rows_first):
        trades = [(rows_of, "x", bit) for bit in reversed(far_bits)]
        trades = [(columns, "z", bit) for bit in bits_of(tracks)] + trades
        if rows_first:
            trades = trades[len(bits_of(tracks)) :] + trades[: len(bits_of(tracks))]
        amount = 1.0 if groups > 1 else 0.5
        out = []
        for (_, link, bit), after in zip(trades, trades[1:] + [None]):
            if link == "z":
                link, load = ("out" if bit == 1 else "mid"), amount * bit
            else:
                load = amount
            amount /= 2
            if after is None:
                step = final
            else:
                step = functools.partial(after[0], bit=after[2])
            out.append((step, (link, load)))
        return out

    plans = []
    for c in range(len(sizes)):
        plans.append(steps + tail(c >= len(sizes) - ROWS_FIRST))
    shares = [size / tok_rows for size in sizes]
    for c in range(len(sizes)):
        begin(c)
    order = order_of(shares, plans, expert)
    if sorted(order) == sorted(TUNED):
        order = TUNED
    for c, at in order:
        plans[c][at][0](c)
    return result[0]


def local(states, routes, route_gates, norm_gain, w_gate, w_up, w_down):
    tok_rows = states.shape[1]
    experts = w_gate.shape[1] * lax.axis_size("expert")
    if 4 * tok_rows // experts < tok_rows or w_gate.shape[1] != 1:
        return dispatched(states, routes, route_gates, norm_gain, w_gate, w_up, w_down)
    return dense(states, routes, route_gates, norm_gain, w_gate, w_up, w_down)


def solution(mesh):
    return jax.shard_map(
        local,
        mesh=mesh,
        in_specs=(
            P("track", ("groups", "expert"), None),
            P("track", ("groups", "expert"), None),
            P("track", ("groups", "expert"), None),
            P("track", None),
            P("track", "expert", None, None),
            P("track", "expert", None, None),
            P("track", "expert", None, None),
        ),
        out_specs=P(("groups", "expert"), "track"),
        check_vma=False,
    )
```
